256 devices in a mesh: ctx: 64 (over x, z, core), head: 4 (over y).
Axes of the slice: x: 4, y: 4, z: 8, core: 2. Of those that a mesh axis runs over, the one named last changes fastest.
Arguments:
- queries: bfloat16 [8192, 8192], P('ctx', 'head'), may hold values from -7 to 7
- span_kv: bfloat16 [8192, 8, 256], P('ctx', 'head'), may hold values from -7 to 7
- cache_kv: bfloat16 [262144, 8, 256], P('ctx', 'head'), may hold values from -6 to 6
- verticals: int32 [8, 64], P('head'), may hold values from 0 to 4095, as said below
- offsets: int32 [8, 8], P('head'), may hold values from 0 to 7, as said below
Outputs:
- attended: bfloat16 [8192, 8192], P(('ctx', 'head'))
The draws below stay inside these ranges and needn't reach their ends.
Inputs may be any that keep to these rules, and one draw needn't show every extreme that they name: `verticals`: each row holds 64 distinct cache blocks. Cache block b lies in the cache of index b // 64 of ctx; at most 2 blocks of one row lie in one index's cache, and in every row some index holds exactly 2. Each row holds 8 distinct offsets, 0 among them; some row holds 7.
All inputs are finite; a program needn't handle non-finite values.
Results may differ from the reference program's by a relative error of at most 0.0065.
Values may be sent and summed in bfloat16 or wider, within the bound.
A program may use at most 192 MiB of HBM per device.

```python
import jax
import jax.numpy as jnp
from jax import lax

QH = 64
KVH = 8
HD = 128
BLK = 64
CACHE_DEV = 4096
NV = 64
NS = 8
VCAP = 2
SMAX = 8
SPAN = 8192
CACHE = 262144
N_CTX = 64


def draw_verticals(key, part):
    owner_total = N_CTX
    per_owner = CACHE_DEV // BLK
    slot_total = owner_total * VCAP

    def one_head(head_key):
        key_one, key_two, key_three, key_four = jax.random.split(head_key, 4)
        full_owner = jax.random.randint(key_one, (), 0, owner_total)
        slot_order = jax.random.permutation(key_two, slot_total)
        priority = jnp.where(slot_order // VCAP == full_owner, 0, 1) * slot_total + jnp.arange(slot_total)
        chosen = slot_order[jnp.argsort(priority)][:NV]
        chosen = chosen[jax.random.permutation(key_four, NV)]
        tables = jax.vmap(lambda table_key: jax.random.permutation(table_key, per_owner))(jax.random.split(key_three, owner_total))
        owner_id = chosen // VCAP
        slot_id = chosen % VCAP
        return (owner_id * per_owner + tables[owner_id, slot_id]).astype(jnp.int32)
    return jax.vmap(one_head)(jax.random.split(key, KVH))


def draw_offsets(key, part):
    key_one, key_two = jax.random.split(key)
    chosen_head = jax.random.randint(key_one, (), 0, KVH)

    def one_head(head_key, head_index):
        key_first, key_second = jax.random.split(head_key)
        chosen_offsets = jax.random.permutation(key_first, SMAX - 1)[:NS - 1] + 1
        forced = jnp.where(jnp.any(chosen_offsets == SMAX - 1), chosen_offsets, chosen_offsets.at[NS - 2].set(SMAX - 1))
        chosen_offsets = jnp.where(head_index == chosen_head, forced, chosen_offsets)
        offset_row = jnp.concatenate([jnp.zeros((1,), jnp.int32), chosen_offsets.astype(jnp.int32)])
        return offset_row[jax.random.permutation(key_second, NS)]
    return jax.vmap(one_head)(jax.random.split(key_two, KVH), jnp.arange(KVH))


def draw_queries(key, part):
    key_one = jax.random.fold_in(jax.random.fold_in(key, 3), 0)
    values_base = jnp.clip(jax.random.normal(key_one, (SPAN, QH, HD)), -6.0, 6.0)
    return values_base.reshape(SPAN, QH * HD).astype(jnp.bfloat16)


def draw_span_kv(key, part):
    key_one = jax.random.fold_in(jax.random.fold_in(key, 5), 0)
    values_base = jnp.clip(jax.random.normal(key_one, (SPAN, KVH, 2 * HD)), -6.0, 6.0)
    return values_base.astype(jnp.bfloat16)


def steps_of(key, shape, shards, least, largest):
    def one(axis_at, parts):
        steps = jax.random.uniform(jax.random.fold_in(jax.random.fold_in(key, 6), axis_at), (parts,), jnp.float32, least / len(shards), largest / len(shards))
        return jnp.repeat(jnp.exp(steps), shape[axis_at] // parts).reshape((-1,) + (1,) * (len(shape) - axis_at - 1))

    factor_of = one(*shards[0])
    for cut in shards[1:]:
        factor_of = factor_of * one(*cut)
    return factor_of


def gaussian(stream_key, dims, deviation, reach, cuts=(), held_as=jnp.bfloat16):
    values = deviation * jax.random.normal(stream_key, dims, jnp.float32)
    if cuts:
        values = values * steps_of(stream_key, dims, cuts, -0.22, 0.18)
    return jnp.clip(values, -reach, reach).astype(held_as)


def setup_inputs(seed: int = 0) -> dict:
    seeds = jax.random.split(jax.random.key(seed), 6)
    return {
        "queries": draw_queries(jax.random.fold_in(seeds[5], 71), 0),
        "span_kv": draw_span_kv(jax.random.fold_in(seeds[5], 71), 0),
        "cache_kv": gaussian(seeds[2], (CACHE, KVH, 2 * HD), 1.0, 6.0, ((0, 64), (1, 4))),
        "verticals": draw_verticals(jax.random.fold_in(seeds[5], 71), 0),
        "offsets": draw_offsets(jax.random.fold_in(seeds[5], 71), 0),
    }


def reference(queries, span_kv, cache_kv, verticals, offsets):
    span_blocks = SPAN // BLK
    group_size = QH // KVH
    score_scale = HD ** -0.5
    cache_blocked = cache_kv.reshape(CACHE // BLK, BLK, KVH, 2 * HD)
    span_blocked = span_kv.reshape(span_blocks, BLK, KVH, 2 * HD)
    query_blocked = queries.reshape(span_blocks, BLK, KVH, group_size, HD)
    causal = jnp.arange(BLK)[None, :] <= jnp.arange(BLK)[:, None]

    def per_head(head_index):
        cache_head = lax.dynamic_index_in_dim(cache_blocked, head_index, 2, False)
        span_head = lax.dynamic_index_in_dim(span_blocked, head_index, 2, False)
        query_head = lax.dynamic_index_in_dim(query_blocked, head_index, 2, False)
        vertical_ids = lax.dynamic_index_in_dim(verticals, head_index, 0, False)
        head_offsets = lax.dynamic_index_in_dim(offsets, head_index, 0, False)
        vertical_rows = jnp.take(cache_head, vertical_ids, axis=0).reshape(NV * BLK, 2 * HD).astype(jnp.float32)

        def per_block(block_index):
            query_block = lax.dynamic_index_in_dim(query_head, block_index, 0, False).astype(jnp.float32)
            source_block = block_index - head_offsets
            source_live = source_block >= 0
            slash_rows = jnp.take(span_head, jnp.maximum(source_block, 0), axis=0).astype(jnp.float32)
            vertical_scores = jnp.einsum("qgd,kd->gqk", query_block, vertical_rows[:, :HD]) * score_scale
            slash_scores = jnp.einsum("qgd,skd->gqsk", query_block, slash_rows[..., :HD]) * score_scale
            allowed = source_live[:, None, None] & ((head_offsets[:, None, None] > 0) | causal[None])
            allowed = jnp.transpose(allowed, (1, 0, 2))
            slash_scores = jnp.where(allowed[None], slash_scores, -jnp.inf)
            row_top = jnp.maximum(jnp.max(vertical_scores, axis=-1), jnp.max(slash_scores, axis=(-2, -1)))
            vertical_weights = jnp.exp(vertical_scores - row_top[..., None])
            slash_weights = jnp.exp(slash_scores - row_top[..., None, None])
            row_total = jnp.sum(vertical_weights, axis=-1) + jnp.sum(slash_weights, axis=(-2, -1))
            weighted = jnp.einsum("gqk,kd->gqd", vertical_weights.astype(jnp.bfloat16).astype(jnp.float32), vertical_rows[:, HD:])
            weighted = weighted + jnp.einsum("gqsk,skd->gqd", slash_weights.astype(jnp.bfloat16).astype(jnp.float32), slash_rows[..., HD:])
            normalized = weighted / row_total[..., None]
            return jnp.transpose(normalized, (1, 0, 2)).astype(jnp.bfloat16)

        return lax.map(per_block, jnp.arange(span_blocks, dtype=jnp.int32))

    result = lax.map(per_head, jnp.arange(KVH, dtype=jnp.int32))
    return jnp.transpose(result, (1, 2, 0, 3, 4)).reshape(SPAN, QH * HD)
```

```python
import jax
import jax.numpy as jnp
from jax import lax
from jax.experimental import pallas as pl
from jax.experimental.pallas import tpu as pltpu
from jax.sharding import PartitionSpec as P

BLK = 64
HD = 128
NX, NZ, NY = 4, 8, 4
CHIPS = NX * NZ
GROUP = 8
TOK = 128
SUB = TOK // NY
ROWS = GROUP * SUB
CHUNKS = 2 * NY
CHUNK_KEYS = 4 * BLK
TILE = NX * CHUNK_KEYS
WINDOW = 6 * TOK
QW = GROUP * HD
FLOOR = -1e30
DEAD = -30000.0
SCALE = float(HD ** -0.5 * 1.4426950408889634)
MESH = pl.DeviceIdType.MESH


def kernel(picks, bias, q_hbm, span_hbm, cache_hbm, out_hbm,
           cache, span, span_heads, staged, gathered, q_own, q_far, window,
           q2, k2, v2, wk, wv, acc, top, slab,
           load_sem, swap_send, swap_recv, halo_send, halo_recv,
           piece_send, piece_recv, out_send, out_recv, own_sem):
    me = lax.axis_index("ctx")
    y = lax.axis_index("head")
    chip = me // 2
    core = me % 2
    other = 1 - core
    x = chip // NZ
    z = chip % NZ

    def at_chip(cx, cz, which):
        return (2 * ((cx % NX) * NZ + cz % NZ) + which, y)

    partner = (2 * chip + other, y)
    x_up, x_down, x_far = (at_chip(x + s, z, core) for s in (1, NX - 1, 2))
    z_up, z_down = (at_chip(x, z + s, core) for s in (1, NZ - 1))

    def linear(step, which):
        return (2 * ((chip + CHIPS + step) % CHIPS) + which, y)

    barrier = pltpu.get_barrier_semaphore()
    peers = [partner, x_up, x_down, x_far, z_up, z_down]
    peers += [linear(s, w) for s in (1, -1, 2, -2) for w in (0, 1)]
    peers += [(2 * chip + w, (y + r) % NY) for r in (1, 2, 3) for w in (0, 1)]
    for peer in peers:
        pl.semaphore_signal(barrier, inc=1, device_id=peer, device_id_type=MESH)

    load_cache = pltpu.make_async_copy(cache_hbm, cache, load_sem.at[0])
    load_span = pltpu.make_async_copy(span_hbm, span, load_sem.at[1])
    own_columns = pl.ds(pl.multiple_of(core * QW, QW), QW)
    far_columns = pl.ds(pl.multiple_of(other * QW, QW), QW)
    load_q = pltpu.make_async_copy(q_hbm.at[:, own_columns], q_own, load_sem.at[2])
    load_span.start()
    load_cache.start()
    load_q.start()

    load_span.wait()
    both = span[...].astype(jnp.float32)
    for head in range(2):
        span_heads[head] = both[:, head, :].astype(jnp.bfloat16)
    load_cache.wait()
    for head in range(2):
        for slot in range(2):
            block = cache[picks[head, slot]].astype(jnp.float32)
            staged[head, slot * BLK:(slot + 1) * BLK, :] = block[:, head, :].astype(jnp.bfloat16)

    mine = pl.ds(pl.multiple_of(core * 2 * BLK, 2 * BLK), 2 * BLK)
    gathered[z, x, mine, :] = staged[core]
    own_rows = pl.ds(pl.multiple_of(4 * TOK + core * TOK, TOK), TOK)
    window[own_rows, :] = span_heads[core]

    pl.semaphore_wait(barrier, len(peers))

    def remote(src, dst, send, recv, device):
        return pltpu.make_async_remote_copy(
            src_ref=src, dst_ref=dst, send_sem=send, recv_sem=recv,
            device_id=device, device_id_type=MESH)

    swaps = [
        remote(staged.at[other], gathered.at[z, x, mine, :], swap_send.at[0], swap_recv.at[0], partner),
        remote(q_hbm.at[:, far_columns], q_far, swap_send.at[1], swap_recv.at[1], partner),
        remote(span_heads.at[other], window.at[own_rows, :], swap_send.at[2], swap_recv.at[2], partner),
    ]
    for swap in swaps:
        swap.start()
    halos = []
    for back in (1, 2):
        rows = pl.ds(pl.multiple_of((2 - back) * 2 * TOK + core * TOK, TOK), TOK)
        for head in range(2):
            halos.append(remote(
                span_heads.at[head], window.at[rows, :],
                halo_send.at[back - 1, head], halo_recv.at[back - 1, core],
                linear(back, head)))

    def row_of(k):
        return (z + NZ + (1 - 2 * (k % 2)) * ((k + 1) // 2)) % NZ

    def piece(k, off, way, device, k_there, off_there):
        src = gathered.at[row_of(k), (x + off) % NX]
        return remote(src, src, piece_send.at[k, off, way],
                      piece_recv.at[k_there, off_there], device)

    def along_z(k, off, act):
        @pl.when(k == 0)
        def _():
            act(piece(k, off, 0, z_up, 1, off))
            act(piece(k, off, 1, z_down, 2, off))

        @pl.when((k % 2 == 1) & (k <= 3))
        def _():
            act(piece(k, off, 0, z_up, k + 2, off))

        @pl.when((k % 2 == 0) & (k >= 2))
        def _():
            act(piece(k, off, 1, z_down, k + 2 - k // 6, off))

    def along_x(k, act):
        act(piece(k, 0, 2, x_up, k, 3))
        act(piece(k, 0, 3, x_down, k, 1))

        @pl.when(k == 0)
        def _():
            act(piece(k, 0, 4, x_far, k, 2))

    def relay_x(k, act):
        @pl.when(k % 2 == 1)
        def _():
            act(piece(k, 3, 2, x_up, k, 2))

        @pl.when((k % 2 == 0) & (k >= 2))
        def _():
            act(piece(k, 1, 3, x_down, k, 2))

    def begin(copy):
        copy.start()

    def drain(copy):
        copy.wait_send()

    def arrive(k, off):
        here = gathered.at[row_of(k), (x + off) % NX]
        remote(here, here, piece_send.at[k, off, 0], piece_recv.at[k, off], partner).wait_recv()

    def stage_a(k):
        arrive(k, 0)
        along_z(k, 0, begin)
        along_x(k, begin)

    def stage_b(k):
        @pl.when(k % 2 == 1)
        def _():
            arrive(k, 3)

        @pl.when(k % 2 == 0)
        def _():
            arrive(k, 1)
        relay_x(k, begin)

    swaps[0].wait_recv()
    along_z(0, 0, begin)
    along_x(0, begin)
    for halo in halos:
        halo.start()

    load_q.wait()
    swaps[1].wait_recv()
    for rel in range(2):
        source = q_own if rel == 0 else q_far
        for r in range(NY):
            first = pl.multiple_of(((y + r) % NY) * SUB, SUB)
            for h in range(GROUP):
                part = source[pl.ds(first, SUB), h * HD:(h + 1) * HD].astype(jnp.float32) * SCALE
                high = part.astype(jnp.bfloat16)
                low = (part - high.astype(jnp.float32)).astype(jnp.bfloat16)
                lane = lax.broadcasted_iota(jnp.int32, (SUB, HD), 1)
                low = jnp.where(lane == HD - 1, jnp.ones_like(low), low)
                base = (rel * NY + r) * ROWS + h * SUB
                q2[base:base + SUB, 0:HD] = high
                q2[base:base + SUB, HD:2 * HD] = low

    acc[...] = jnp.zeros_like(acc)
    top[...] = jnp.full_like(top, FLOOR)
    v2[:, HD:2 * HD] = jnp.ones((TILE, HD), jnp.bfloat16)
    wv[:, HD:2 * HD] = jnp.ones((WINDOW, HD), jnp.bfloat16)

    def update(n, scores, values):
        rows = slice(n * ROWS, (n + 1) * ROWS)
        before = top[rows, :]
        now = jnp.maximum(before, jnp.max(scores, axis=1, keepdims=True))
        weights = jnp.exp2(scores - now[:, 0:1]).astype(jnp.bfloat16)
        added = jnp.dot(weights, values, preferred_element_type=jnp.float32)
        keep = jnp.exp2(before - now)
        top[rows, :] = now
        acc[rows, 0:HD] = acc[rows, 0:HD] * keep + added[:, 0:HD]
        acc[rows, HD:2 * HD] = acc[rows, HD:2 * HD] * keep + added[:, HD:2 * HD]

    def score(n, keys):
        return lax.dot_general(
            q2[n * ROWS:(n + 1) * ROWS, :], keys, (((1,), (1,)), ((), ())),
            preferred_element_type=jnp.float32)

    def slash():
        for back in (1, 2):
            for which in range(2):
                rows = window.at[(2 - back) * 2 * TOK + which * TOK:(2 - back) * 2 * TOK + (which + 1) * TOK, :]
                remote(rows, rows, halo_send.at[back - 1, 0], halo_recv.at[back - 1, which], partner).wait_recv()
        swaps[2].wait_recv()
        wk[:, 0:HD] = window[:, 0:HD]
        lane = lax.broadcasted_iota(jnp.int32, (WINDOW, HD), 1)
        wk[:, HD:2 * HD] = jnp.where(lane == HD - 1, jnp.zeros((WINDOW, HD), jnp.bfloat16), window[:, 0:HD])
        wv[:, 0:HD] = window[:, HD:2 * HD]
        for n in range(CHUNKS):
            place = core if n < NY else other
            first = ((y + n % NY) % NY) * SUB
            block = 2 * place + first // BLK
            keys = pl.ds(pl.multiple_of((block + 1) * BLK, BLK), 8 * BLK)
            column = lax.broadcasted_iota(jnp.int32, (ROWS, 8 * BLK), 1)
            token = lax.broadcasted_iota(jnp.int32, (ROWS, 8 * BLK), 0) % SUB + first % BLK
            allowed = (column <= 7 * BLK + token) & (column >= (7 - block - 4 * chip) * BLK)
            scores = jnp.where(allowed, score(n, wk[keys, :]), FLOOR)
            update(n, scores, wv[keys, :])

    def tile(k):
        row = row_of(k)
        lane = lax.broadcasted_iota(jnp.int32, (BLK, HD), 1)
        for cx in range(NX):
            for b in range(4):
                owner = 2 * (cx * NZ + row) + b // 2
                fill = jnp.full((BLK, HD), bias[core, 2 * owner + b % 2], jnp.float32)
                rows = slice(b * BLK, (b + 1) * BLK)
                there = slice(cx * CHUNK_KEYS + b * BLK, cx * CHUNK_KEYS + (b + 1) * BLK)
                keys = gathered[row, cx, rows, 0:HD]
                k2[there, 0:HD] = keys
                k2[there, HD:2 * HD] = jnp.where(lane == HD - 1, fill.astype(jnp.bfloat16), keys)
                v2[there, 0:HD] = gathered[row, cx, rows, HD:2 * HD]
        for n in range(CHUNKS):
            update(n, score(n, k2[...]), v2[...])

    @pl.when(core == 1)
    def _():
        stage_a(1)

    def step(k, carry):
        @pl.when(core == 0)
        def _():
            @pl.when(k > 0)
            def _():
                arrive(k, 0)
                along_z(k, 0, begin)
            for off in (1, 3, 2):
                arrive(k, off)
                along_z(k, off, begin)

        @pl.when(core == 1)
        def _():
            @pl.when(k + 2 < NZ)
            def _():
                stage_a(k + 2)

            @pl.when(k + 1 < NZ)
            def _():
                stage_b(k + 1)

            @pl.when((k == 0) | (k % 2 == 1))
            def _():
                arrive(k, 1)

            @pl.when(k % 2 == 0)
            def _():
                arrive(k, 3)
            arrive(k, 2)
        tile(k)

        @pl.when(k == 0)
        def _():
            slash()
        return carry

    lax.fori_loop(0, NZ, step, 0)

    out_columns = pl.ds(pl.multiple_of(y * 2 * QW + core * QW, QW), QW)
    sends = []
    keep_own = pltpu.make_async_copy(slab.at[0], out_hbm.at[:, out_columns], own_sem)
    for n in (2, 6, 1, 5, 3, 7, 4, 0):
        rows = slice(n * ROWS, (n + 1) * ROWS)
        done = (acc[rows, 0:HD] / acc[rows, HD:2 * HD]).astype(jnp.bfloat16)
        for h in range(GROUP):
            slab[n, :, h * HD:(h + 1) * HD] = done[h * SUB:(h + 1) * SUB, :]
        if n == 0:
            keep_own.start()
        else:
            place = core if n < NY else other
            send = remote(slab.at[n], out_hbm.at[:, out_columns], out_send.at[n], out_recv.at[n],
                          (2 * chip + place, (y + n % NY) % NY))
            send.start()
            sends.append(send)

    for swap in swaps:
        swap.wait_send()
    for halo in halos:
        halo.wait_send()

    def finish(k, carry):
        along_z(k, 0, drain)

        @pl.when(core == 0)
        def _():
            for off in (1, 2, 3):
                along_z(k, off, drain)

            @pl.when(k == 0)
            def _():
                along_x(k, drain)

        @pl.when(core == 1)
        def _():
            along_x(k, drain)
            relay_x(k, drain)
        return carry

    lax.fori_loop(0, NZ, finish, 0)
    for send in sends:
        send.wait()
    keep_own.wait()


def body(queries, span_kv, cache_kv, verticals, offsets):
    heads = span_kv.shape[1]
    owners = lax.axis_size("ctx")
    my_index = lax.axis_index("ctx")
    cache_blocks = cache_kv.shape[0] // BLK
    owner_of = verticals // cache_blocks
    in_owner = verticals % cache_blocks
    is_mine = owner_of == my_index
    rank = jnp.cumsum(is_mine.astype(jnp.int32), axis=1) - 1
    slots = jnp.arange(2, dtype=jnp.int32)
    hit = is_mine[:, None, :] & (rank[:, None, :] == slots[None, :, None])
    picks = jnp.sum(jnp.where(hit, in_owner[:, None, :], 0), axis=2)
    held = jnp.sum(
        (owner_of[:, None, :] == jnp.arange(owners, dtype=jnp.int32)[None, :, None]).astype(jnp.int32),
        axis=2)
    bias = jnp.where(slots[None, None, :] < held[:, :, None], 0.0, DEAD).astype(jnp.float32)
    bias = bias.reshape(heads, 2 * owners)
    bf16 = jnp.bfloat16
    any_space = pl.BlockSpec(memory_space=pl.ANY)
    smem = pl.BlockSpec(memory_space=pltpu.SMEM)
    dma = pltpu.SemaphoreType.DMA
    return pl.pallas_call(
        kernel,
        out_shape=jax.ShapeDtypeStruct((SUB, 4 * 2 * QW), bf16),
        in_specs=[smem, smem, any_space, any_space, any_space],
        out_specs=any_space,
        scratch_shapes=[
            pltpu.VMEM((cache_blocks, BLK) + cache_kv.shape[1:], bf16),
            pltpu.VMEM(span_kv.shape, bf16),
            pltpu.VMEM((2, TOK, 2 * HD), bf16),
            pltpu.VMEM((2, 2 * BLK, 2 * HD), bf16),
            pltpu.VMEM((NZ, NX, CHUNK_KEYS, 2 * HD), bf16),
            pltpu.VMEM((TOK, QW), bf16),
            pltpu.VMEM((TOK, QW), bf16),
            pltpu.VMEM((WINDOW, 2 * HD), bf16),
            pltpu.VMEM((CHUNKS * ROWS, 2 * HD), bf16),
            pltpu.VMEM((TILE, 2 * HD), bf16),
            pltpu.VMEM((TILE, 2 * HD), bf16),
            pltpu.VMEM((WINDOW, 2 * HD), bf16),
            pltpu.VMEM((WINDOW, 2 * HD), bf16),
            pltpu.VMEM((CHUNKS * ROWS, 2 * HD), jnp.float32),
            pltpu.VMEM((CHUNKS * ROWS, HD), jnp.float32),
            pltpu.VMEM((CHUNKS, SUB, QW), bf16),
            dma((3,)), dma((3,)), dma((3,)), dma((2, 2)), dma((2, 2)),
            dma((NZ, NX, 5)), dma((NZ, NX)), dma((CHUNKS,)), dma((CHUNKS,)), dma,
        ],
        compiler_params=pltpu.CompilerParams(
            collective_id=0, has_side_effects=True, vmem_limit_bytes=60 << 20),
    )(picks, bias, queries, span_kv, cache_kv.reshape((cache_blocks, BLK) + cache_kv.shape[1:]))


def solution(mesh):
    in_specs = (
        P("ctx", "head"),
        P("ctx", "head", None),
        P("ctx", "head", None),
        P("head", None),
        P("head", None),
    )
    out_specs = P(("ctx", "head"), None)
    return jax.shard_map(body, mesh=mesh, in_specs=in_specs, out_specs=out_specs, check_vma=False)
```

```python
import jax
import jax.numpy as jnp
from jax import lax
from jax.experimental import pallas as pl
from jax.experimental.pallas import tpu as pltpu
from jax.sharding import PartitionSpec as P

BLK = 64
HD = 128
NX, NZ, NY = 4, 8, 4
CHIPS = NX * NZ
GROUP = 8
TOK = 128
SUB = TOK // NY
ROWS = GROUP * SUB
CHUNKS = 2 * NY
CHUNK_KEYS = 4 * BLK
TILE = NX * CHUNK_KEYS
FAR = 2 * TOK
WINDOW = 3 * FAR
NV = 64
QW = GROUP * HD
FLOOR = -1e30
DEAD = -30000.0
SCALE = float(HD ** -0.5 * 1.4426950408889634)
MESH = pl.DeviceIdType.MESH


def kernel(verts_hbm, q_hbm, span_hbm, cache_hbm, out_hbm,
           verts, bias, cache, span, span_heads, staged, gathered, q_own, q_far, window,
           q2, k2, v2, wk, wv, acc, top, slab,
           load_sem, swap_send, swap_recv, halo_send, halo_recv, ready,
           piece_send, piece_recv, out_send, out_recv, own_sem):
    me = lax.axis_index("ctx")
    y = lax.axis_index("head")
    chip = me // 2
    core = me % 2
    other = 1 - core
    x = chip // NZ
    z = chip % NZ

    def at_chip(cx, cz, which):
        return (2 * ((cx % NX) * NZ + cz % NZ) + which, y)

    partner = (2 * chip + other, y)
    x_up, x_down, x_far = (at_chip(x + s, z, core) for s in (1, NX - 1, 2))
    z_up, z_down = (at_chip(x, z + s, core) for s in (1, NZ - 1))
    after, before_it = ((2 * ((chip + CHIPS + s) % CHIPS) + core, y) for s in (1, -1))

    load_verts = pltpu.make_async_copy(verts_hbm, verts, load_sem.at[3])
    load_verts.start()
    barrier = pltpu.get_barrier_semaphore()
    peers = [partner, x_up, x_down, z_up, z_down, after, before_it]
    peers += [(2 * chip + w, (y + r) % NY) for r in (1, 3) for w in (0, 1)]
    for peer in peers:
        pl.semaphore_signal(barrier, inc=1, device_id=peer, device_id_type=MESH)

    load_cache = pltpu.make_async_copy(cache_hbm, cache, load_sem.at[0])
    load_span = pltpu.make_async_copy(span_hbm, span, load_sem.at[1])
    own_columns = pl.ds(pl.multiple_of(core * QW, QW), QW)
    far_columns = pl.ds(pl.multiple_of(other * QW, QW), QW)
    load_q = pltpu.make_async_copy(q_hbm.at[:, own_columns], q_own, load_sem.at[2])
    load_span.start()
    load_cache.start()
    load_q.start()

    load_verts.wait()
    mine_at = (verts[...] // BLK) == me
    within = verts[...] % BLK
    most = jnp.where(mine_at, within, 0)
    least = jnp.where(mine_at, within, BLK - 1)
    owner_row = verts[pl.ds(core, 1), :] // BLK
    owner_index = lax.broadcasted_iota(jnp.int32, (2 * CHIPS, NV), 0)
    held = jnp.sum(jnp.where(owner_index == owner_row, 1.0, 0.0), axis=1, keepdims=True)
    for slot in range(2):
        dead = jnp.where(held > slot + 0.5, 0.0, DEAD)
        bias[slot] = jnp.broadcast_to(dead, (2 * CHIPS, HD))
    load_span.wait()
    both = span[...].astype(jnp.float32)
    for head in range(2):
        span_heads[head] = both[:, head, :].astype(jnp.bfloat16)
    load_cache.wait()
    for head in range(2):
        for slot in range(2):
            pick = jnp.max(most[head:head + 1]) if slot == 0 else jnp.min(least[head:head + 1])
            block = cache[pick].astype(jnp.float32)
            staged[head, slot * BLK:(slot + 1) * BLK, :] = block[:, head, :].astype(jnp.bfloat16)

    mine = pl.ds(pl.multiple_of(core * 2 * BLK, 2 * BLK), 2 * BLK)
    gathered[z, x, mine, :] = staged[core]
    own_rows = pl.ds(pl.multiple_of(4 * TOK + core * TOK, TOK), TOK)
    window[own_rows, :] = span_heads[core]

    pl.semaphore_wait(barrier, len(peers))
    pl.semaphore_signal(ready.at[0], inc=1, device_id=x_up, device_id_type=MESH)
    pl.semaphore_signal(ready.at[1], inc=1, device_id=(me, (y + 1) % NY), device_id_type=MESH)

    def remote(src, dst, send, recv, device):
        return pltpu.make_async_remote_copy(
            src_ref=src, dst_ref=dst, send_sem=send, recv_sem=recv,
            device_id=device, device_id_type=MESH)

    swaps = [
        remote(staged.at[other], gathered.at[z, x, mine, :], swap_send.at[0], swap_recv.at[0], partner),
        remote(q_hbm.at[:, far_columns], q_far, swap_send.at[1], swap_recv.at[1], partner),
        remote(span_heads.at[other], window.at[own_rows, :], swap_send.at[2], swap_recv.at[2], partner),
    ]
    for swap in swaps:
        swap.start()
    halos = [
        remote(window.at[2 * FAR:3 * FAR, :], window.at[FAR:2 * FAR, :],
               halo_send.at[0], halo_recv.at[0], after),
        remote(window.at[FAR + BLK:2 * FAR, :], window.at[BLK:FAR, :],
               halo_send.at[1], halo_recv.at[1], after),
    ]

    def row_of(k):
        return (z + NZ + (1 - 2 * (k % 2)) * ((k + 1) // 2)) % NZ

    def piece(k, off, way, device, k_there, off_there):
        src = gathered.at[row_of(k), (x + off) % NX]
        return remote(src, src, piece_send.at[k, off, way],
                      piece_recv.at[k_there, off_there], device)

    def along_z(k, off, act):
        last_up, last_down = (3, 6) if off == 0 else (1, 4)

        @pl.when(k == 0)
        def _():
            act(piece(k, off, 0, z_up, 1, off))
            act(piece(k, off, 1, z_down, 2, off))

        @pl.when((k % 2 == 1) & (k <= last_up))
        def _():
            act(piece(k, off, 0, z_up, k + 2, off))

        @pl.when((k % 2 == 0) & (k >= 2) & (k <= last_down))
        def _():
            act(piece(k, off, 1, z_down, k + 2 - k // 6, off))

    def along_x(k, act):
        act(piece(k, 0, 2, x_up, k, 3))
        act(piece(k, 0, 3, x_down, k, 1))

        @pl.when(k == 0)
        def _():
            act(piece(k, 0, 4, x_far, k, 2))

    def relays_up(k):
        return (k % 2 == 1) & (k < 7)

    def relays_down(k):
        return ((k % 2 == 0) & (k >= 2)) | (k == 7)

    def relay_x(k, act):
        @pl.when(relays_up(k))
        def _():
            act(piece(k, 3, 2, x_up, k, 2))

        @pl.when(relays_down(k))
        def _():
            act(piece(k, 1, 3, x_down, k, 2))

    def column_first(k):
        return (core == 1) | (k == 5) | (k == 7)

    def begin(copy):
        copy.start()

    def drain(copy):
        copy.wait_send()

    def arrive(k, off):
        here = gathered.at[row_of(k), (x + off) % NX]
        remote(here, here, piece_send.at[k, off, 0], piece_recv.at[k, off], partner).wait_recv()

    def stage_a(k):
        arrive(k, 0)
        along_z(k, 0, begin)

        @pl.when(column_first(k))
        def _():
            along_x(k, begin)

    def stage_b(k):
        @pl.when(column_first(k))
        def _():
            @pl.when(relays_up(k))
            def _():
                arrive(k, 3)

            @pl.when(relays_down(k))
            def _():
                arrive(k, 1)
            relay_x(k, begin)

    def stage_c(k):
        @pl.when(column_first(k))
        def _():
            @pl.when((k == 0) | relays_up(k))
            def _():
                arrive(k, 1)

            @pl.when((k == 0) | relays_down(k))
            def _():
                arrive(k, 3)
            arrive(k, 2)

        @pl.when(jnp.logical_not(column_first(k)))
        def _():
            for off in (1, 3, 2):
                arrive(k, off)
                along_z(k, off, begin)

    swaps[0].wait_recv()
    pl.semaphore_wait(ready.at[0], 1)
    along_z(0, 0, begin)
    along_x(0, begin)
    swaps[2].wait_recv()
    halos[0].start()

    load_q.wait()
    swaps[1].wait_recv()
    for rel in range(2):
        source = q_own if rel == 0 else q_far
        for r in range(NY):
            first = pl.multiple_of(((y + r) % NY) * SUB, SUB)
            for h in range(GROUP):
                part = source[pl.ds(first, SUB), h * HD:(h + 1) * HD].astype(jnp.float32) * SCALE
                high = part.astype(jnp.bfloat16)
                low = (part - high.astype(jnp.float32)).astype(jnp.bfloat16)
                lane = lax.broadcasted_iota(jnp.int32, (SUB, HD), 1)
                low = jnp.where(lane == HD - 1, jnp.ones_like(low), low)
                base = (rel * NY + r) * ROWS + h * SUB
                q2[base:base + SUB, 0:HD] = high
                q2[base:base + SUB, HD:2 * HD] = low

    acc[...] = jnp.zeros_like(acc)
    top[...] = jnp.full_like(top, FLOOR)
    v2[:, HD:2 * HD] = jnp.ones((TILE, HD), jnp.bfloat16)
    wv[:, HD:2 * HD] = jnp.ones((WINDOW, HD), jnp.bfloat16)

    def update(n, scores, values):
        rows = slice(n * ROWS, (n + 1) * ROWS)
        before = top[rows, :]
        now = jnp.maximum(before, jnp.max(scores, axis=1, keepdims=True))
        weights = jnp.exp2(scores - now[:, 0:1]).astype(jnp.bfloat16)
        added = jnp.dot(weights, values, preferred_element_type=jnp.float32)
        keep = jnp.exp2(before - now)
        top[rows, :] = now
        acc[rows, 0:HD] = acc[rows, 0:HD] * keep + added[:, 0:HD]
        acc[rows, HD:2 * HD] = acc[rows, HD:2 * HD] * keep + added[:, HD:2 * HD]

    def score(n, keys):
        return lax.dot_general(
            q2[n * ROWS:(n + 1) * ROWS, :], keys, (((1,), (1,)), ((), ())),
            preferred_element_type=jnp.float32)

    def slash():
        halos[1].wait_recv()
        rows = slice(BLK, WINDOW)
        wk[rows, 0:HD] = window[rows, 0:HD]
        lane = lax.broadcasted_iota(jnp.int32, (WINDOW - BLK, HD), 1)
        wk[rows, HD:2 * HD] = jnp.where(
            lane == HD - 1, jnp.zeros((WINDOW - BLK, HD), jnp.bfloat16), window[rows, 0:HD])
        wv[rows, 0:HD] = window[rows, HD:2 * HD]
        for n in range(CHUNKS):
            place = core if n < NY else other
            first = ((y + n % NY) % NY) * SUB
            block = 2 * place + first // BLK
            keys = pl.ds(pl.multiple_of((block + 1) * BLK, BLK), 8 * BLK)
            column = lax.broadcasted_iota(jnp.int32, (ROWS, 8 * BLK), 1)
            token = lax.broadcasted_iota(jnp.int32, (ROWS, 8 * BLK), 0) % SUB + first % BLK
            allowed = (column <= 7 * BLK + token) & (column >= (7 - block - 4 * chip) * BLK)
            scores = jnp.where(allowed, score(n, wk[keys, :]), FLOOR)
            update(n, scores, wv[keys, :])

    def load_tile(k):
        row = row_of(k)
        lane = lax.broadcasted_iota(jnp.int32, (BLK, HD), 1)
        for cx in range(NX):
            for b in range(4):
                owner = 2 * (cx * NZ + row) + b // 2
                fill = jnp.broadcast_to(bias[b % 2, pl.ds(owner, 1), :], (BLK, HD))
                rows = slice(b * BLK, (b + 1) * BLK)
                there = slice(cx * CHUNK_KEYS + b * BLK, cx * CHUNK_KEYS + (b + 1) * BLK)
                keys = gathered[row, cx, rows, 0:HD]
                k2[there, 0:HD] = keys
                k2[there, HD:2 * HD] = jnp.where(lane == HD - 1, fill.astype(jnp.bfloat16), keys)
                v2[there, 0:HD] = gathered[row, cx, rows, HD:2 * HD]

    stage_a(1)
    halos[0].wait_recv()
    halos[1].start()

    def step(k, carry):
        @pl.when(k + 2 < NZ)
        def _():
            stage_a(k + 2)

        stage_b(k + 1)
        stage_c(k)
        load_tile(k)
        for n in range(CHUNKS):
            update(n, score(n, k2[...]), v2[...])

        @pl.when(k == 0)
        def _():
            slash()
        return carry

    lax.fori_loop(0, NZ - 1, step, 0)
    stage_c(NZ - 1)
    load_tile(NZ - 1)
    pl.semaphore_wait(ready.at[1], 1)

    out_columns = pl.ds(pl.multiple_of(y * 2 * QW + core * QW, QW), QW)
    sends = []
    keep_own = pltpu.make_async_copy(slab.at[0], out_hbm.at[:, out_columns], own_sem)
    for n in (2, 6, 1, 5, 3, 7, 4, 0):
        update(n, score(n, k2[...]), v2[...])
        rows = slice(n * ROWS, (n + 1) * ROWS)
        done = (acc[rows, 0:HD] / acc[rows, HD:2 * HD]).astype(jnp.bfloat16)
        for h in range(GROUP):
            slab[n, :, h * HD:(h + 1) * HD] = done[h * SUB:(h + 1) * SUB, :]
        if n == 0:
            keep_own.start()
        else:
            place = core if n < NY else other
            send = remote(slab.at[n], out_hbm.at[:, out_columns], out_send.at[n], out_recv.at[n],
                          (2 * chip + place, (y + n % NY) % NY))
            send.start()
            sends.append(send)

    for swap in swaps:
        swap.wait_send()
    for halo in halos:
        halo.wait_send()

    def finish(k, carry):
        along_z(k, 0, drain)

        @pl.when((k == 0) | column_first(k))
        def _():
            along_x(k, drain)

        @pl.when(column_first(k))
        def _():
            relay_x(k, drain)

        @pl.when(jnp.logical_not(column_first(k)))
        def _():
            for off in (1, 2, 3):
                along_z(k, off, drain)
        return carry

    lax.fori_loop(0, NZ, finish, 0)
    for send in sends:
        send.wait()
    keep_own.wait()


def body(queries, span_kv, cache_kv, verticals, offsets):
    cache_blocks = cache_kv.shape[0] // BLK
    bf16 = jnp.bfloat16
    any_space = pl.BlockSpec(memory_space=pl.ANY)
    dma = pltpu.SemaphoreType.DMA
    return pl.pallas_call(
        kernel,
        out_shape=jax.ShapeDtypeStruct((SUB, 4 * 2 * QW), bf16),
        in_specs=[any_space] * 4,
        out_specs=any_space,
        scratch_shapes=[
            pltpu.VMEM((2, NV), jnp.int32),
            pltpu.VMEM((2, 2 * CHIPS, HD), jnp.float32),
            pltpu.VMEM((cache_blocks, BLK) + cache_kv.shape[1:], bf16),
            pltpu.VMEM(span_kv.shape, bf16),
            pltpu.VMEM((2, TOK, 2 * HD), bf16),
            pltpu.VMEM((2, 2 * BLK, 2 * HD), bf16),
            pltpu.VMEM((NZ, NX, CHUNK_KEYS, 2 * HD), bf16),
            pltpu.VMEM((TOK, QW), bf16),
            pltpu.VMEM((TOK, QW), bf16),
            pltpu.VMEM((WINDOW, 2 * HD), bf16),
            pltpu.VMEM((CHUNKS * ROWS, 2 * HD), bf16),
            pltpu.VMEM((TILE, 2 * HD), bf16),
            pltpu.VMEM((TILE, 2 * HD), bf16),
            pltpu.VMEM((WINDOW, 2 * HD), bf16),
            pltpu.VMEM((WINDOW, 2 * HD), bf16),
            pltpu.VMEM((CHUNKS * ROWS, 2 * HD), jnp.float32),
            pltpu.VMEM((CHUNKS * ROWS, HD), jnp.float32),
            pltpu.VMEM((CHUNKS, SUB, QW), bf16),
            dma((4,)), dma((3,)), dma((3,)), dma((2,)), dma((2,)), pltpu.SemaphoreType.REGULAR((2,)),
            dma((NZ, NX, 5)), dma((NZ, NX)), dma((CHUNKS,)), dma((CHUNKS,)), dma,
        ],
        compiler_params=pltpu.CompilerParams(
            collective_id=0, has_side_effects=True, vmem_limit_bytes=60 << 20),
    )(verticals, queries, span_kv, cache_kv.reshape((cache_blocks, BLK) + cache_kv.shape[1:]))


def solution(mesh):
    in_specs = (
        P("ctx", "head"),
        P("ctx", "head", None),
        P("ctx", "head", None),
        P("head", None),
        P("head", None),
    )
    out_specs = P(("ctx", "head"), None)
    return jax.shard_map(body, mesh=mesh, in_specs=in_specs, out_specs=out_specs, check_vma=False)
```

```python
import jax
import jax.numpy as jnp
from jax import lax
from jax.experimental import pallas as pl
from jax.experimental.pallas import tpu as pltpu
from jax.sharding import PartitionSpec as P

BLK = 64
HD = 128
NX, NZ, NY = 4, 8, 4
CHIPS = NX * NZ
GROUP = 8
TOK = 128
SUB = TOK // NY
ROWS = GROUP * SUB
CHUNKS = 2 * NY
CHUNK_KEYS = 4 * BLK
TILE = NX * CHUNK_KEYS
FAR = 2 * TOK
WINDOW = 3 * FAR
NV = 64
HALO_AT, RELAY_AT = 0, 2
QW = GROUP * HD
FLOOR = -1e30
DEAD = -30000.0
SCALE = float(HD ** -0.5 * 1.4426950408889634)
MESH = pl.DeviceIdType.MESH


def kernel(verts_hbm, q_hbm, span_hbm, cache_hbm, out_hbm,
           verts, bias, cache, span, span_heads, staged, gathered, q_own, q_far, window,
           q2, k2, v2, wk, wv, acc, top, slab,
           load_sem, swap_send, swap_recv, halo_send, halo_recv, ready,
           piece_send, piece_recv, out_send, out_recv, own_sem):
    me = lax.axis_index("ctx")
    y = lax.axis_index("head")
    chip = me // 2
    core = me % 2
    other = 1 - core
    x = chip // NZ
    z = chip % NZ

    def at_chip(cx, cz, which):
        return (2 * ((cx % NX) * NZ + cz % NZ) + which, y)

    partner = (2 * chip + other, y)
    x_up, x_down, x_far = (at_chip(x + s, z, core) for s in (1, NX - 1, 2))
    z_up, z_down = (at_chip(x, z + s, core) for s in (1, NZ - 1))
    after, before_it = ((2 * ((chip + CHIPS + s) % CHIPS) + core, y) for s in (1, -1))

    load_verts = pltpu.make_async_copy(verts_hbm, verts, load_sem.at[3])
    load_verts.start()
    barrier = pltpu.get_barrier_semaphore()
    peers = [partner, x_up, x_down, z_up, z_down, after, before_it]
    peers += [(2 * chip + w, (y + r) % NY) for r in (1, 3) for w in (0, 1)]
    for peer in peers:
        pl.semaphore_signal(barrier, inc=1, device_id=peer, device_id_type=MESH)

    load_cache = pltpu.make_async_copy(cache_hbm, cache, load_sem.at[0])
    load_span = pltpu.make_async_copy(span_hbm, span, load_sem.at[1])
    own_columns = pl.ds(pl.multiple_of(core * QW, QW), QW)
    far_columns = pl.ds(pl.multiple_of(other * QW, QW), QW)
    load_q = pltpu.make_async_copy(q_hbm.at[:, own_columns], q_own, load_sem.at[2])
    load_span.start()
    load_cache.start()
    load_q.start()

    load_verts.wait()
    mine_at = (verts[...] // BLK) == me
    within = verts[...] % BLK
    most = jnp.where(mine_at, within, 0)
    least = jnp.where(mine_at, within, BLK - 1)
    owner_row = verts[pl.ds(core, 1), :] // BLK
    owner_index = lax.broadcasted_iota(jnp.int32, (2 * CHIPS, NV), 0)
    held = jnp.sum(jnp.where(owner_index == owner_row, 1.0, 0.0), axis=1, keepdims=True)
    for slot in range(2):
        dead = jnp.where(held > slot + 0.5, 0.0, DEAD)
        bias[slot] = jnp.broadcast_to(dead, (2 * CHIPS, HD))
    load_span.wait()
    both = span[...].astype(jnp.float32)
    for head in range(2):
        span_heads[head] = both[:, head, :].astype(jnp.bfloat16)
    load_cache.wait()
    for head in range(2):
        for slot in range(2):
            pick = jnp.max(most[head:head + 1]) if slot == 0 else jnp.min(least[head:head + 1])
            block = cache[pick].astype(jnp.float32)
            staged[head, slot * BLK:(slot + 1) * BLK, :] = block[:, head, :].astype(jnp.bfloat16)

    mine = pl.ds(pl.multiple_of(core * 2 * BLK, 2 * BLK), 2 * BLK)
    gathered[z, x, mine, :] = staged[core]
    own_rows = pl.ds(pl.multiple_of(4 * TOK + core * TOK, TOK), TOK)
    window[own_rows, :] = span_heads[core]

    pl.semaphore_wait(barrier, len(peers))
    pl.semaphore_signal(ready.at[0], inc=1, device_id=x_up, device_id_type=MESH)
    pl.semaphore_signal(ready.at[1], inc=1, device_id=(me, (y + 1) % NY), device_id_type=MESH)

    def remote(src, dst, send, recv, device):
        return pltpu.make_async_remote_copy(
            src_ref=src, dst_ref=dst, send_sem=send, recv_sem=recv,
            device_id=device, device_id_type=MESH)

    swaps = [
        remote(staged.at[other], gathered.at[z, x, mine, :], swap_send.at[0], swap_recv.at[0], partner),
        remote(q_hbm.at[:, far_columns], q_far, swap_send.at[1], swap_recv.at[1], partner),
        remote(span_heads.at[other], window.at[own_rows, :], swap_send.at[2], swap_recv.at[2], partner),
    ]
    for swap in swaps:
        swap.start()
    halos = [
        remote(window.at[2 * FAR:3 * FAR, :], window.at[FAR:2 * FAR, :],
               halo_send.at[0], halo_recv.at[0], after),
        remote(window.at[FAR + BLK:2 * FAR, :], window.at[BLK:FAR, :],
               halo_send.at[1], halo_recv.at[1], after),
    ]

    def row_of(k):
        return (z + NZ + (1 - 2 * (k % 2)) * ((k + 1) // 2)) % NZ

    def piece(k, off, way, device, k_there, off_there):
        src = gathered.at[row_of(k), (x + off) % NX]
        return remote(src, src, piece_send.at[k, off, way],
                      piece_recv.at[k_there, off_there], device)

    def along_z(k, off, act):
        last_up, last_down = (3, 6) if off == 0 else (1, 4)

        @pl.when(k == 0)
        def _():
            act(piece(k, off, 0, z_up, 1, off))
            act(piece(k, off, 1, z_down, 2, off))

        @pl.when((k % 2 == 1) & (k <= last_up))
        def _():
            act(piece(k, off, 0, z_up, k + 2, off))

        @pl.when((k % 2 == 0) & (k >= 2) & (k <= last_down))
        def _():
            act(piece(k, off, 1, z_down, k + 2 - k // 6, off))

    def along_x(k, act):
        act(piece(k, 0, 2, x_up, k, 3))
        act(piece(k, 0, 3, x_down, k, 1))

        @pl.when(k == 0)
        def _():
            act(piece(k, 0, 4, x_far, k, 2))

    def relays_up(k):
        return (k % 2 == 1) & (k < 7)

    def relays_down(k):
        return ((k % 2 == 0) & (k >= 2)) | (k == 7)

    def relay_x(k, act):
        @pl.when(relays_up(k))
        def _():
            act(piece(k, 3, 2, x_up, k, 2))

        @pl.when(relays_down(k))
        def _():
            act(piece(k, 1, 3, x_down, k, 2))

    def column_first(k):
        return (core == 1) | (k == 5) | (k == 7)

    def begin(copy):
        copy.start()

    def drain(copy):
        copy.wait_send()

    def arrive(k, off):
        here = gathered.at[row_of(k), (x + off) % NX]
        remote(here, here, piece_send.at[k, off, 0], piece_recv.at[k, off], partner).wait_recv()

    def stage_a(k):
        arrive(k, 0)
        along_z(k, 0, begin)

        @pl.when(column_first(k))
        def _():
            along_x(k, begin)

    def stage_b(k):
        @pl.when(column_first(k))
        def _():
            @pl.when(relays_up(k))
            def _():
                arrive(k, 3)

            @pl.when(relays_down(k))
            def _():
                arrive(k, 1)
            relay_x(k, begin)

    def stage_c(k):
        @pl.when(column_first(k))
        def _():
            @pl.when((k == 0) | relays_up(k))
            def _():
                arrive(k, 1)

            @pl.when((k == 0) | relays_down(k))
            def _():
                arrive(k, 3)
            arrive(k, 2)

        @pl.when(jnp.logical_not(column_first(k)))
        def _():
            for off in (1, 3, 2):
                arrive(k, off)
                along_z(k, off, begin)

    swaps[0].wait_recv()
    pl.semaphore_wait(ready.at[0], 1)
    along_z(0, 0, begin)
    along_x(0, begin)

    load_q.wait()
    swaps[1].wait_recv()
    for rel in range(2):
        source = q_own if rel == 0 else q_far
        for r in range(NY):
            first = pl.multiple_of(((y + r) % NY) * SUB, SUB)
            for h in range(GROUP):
                part = source[pl.ds(first, SUB), h * HD:(h + 1) * HD].astype(jnp.float32) * SCALE
                high = part.astype(jnp.bfloat16)
                low = (part - high.astype(jnp.float32)).astype(jnp.bfloat16)
                lane = lax.broadcasted_iota(jnp.int32, (SUB, HD), 1)
                low = jnp.where(lane == HD - 1, jnp.ones_like(low), low)
                base = (rel * NY + r) * ROWS + h * SUB
                q2[base:base + SUB, 0:HD] = high
                q2[base:base + SUB, HD:2 * HD] = low

    acc[...] = jnp.zeros_like(acc)
    top[...] = jnp.full_like(top, FLOOR)
    v2[:, HD:2 * HD] = jnp.ones((TILE, HD), jnp.bfloat16)
    wv[:, HD:2 * HD] = jnp.ones((WINDOW, HD), jnp.bfloat16)

    def update(n, scores, values):
        rows = slice(n * ROWS, (n + 1) * ROWS)
        before = top[rows, :]
        now = jnp.maximum(before, jnp.max(scores, axis=1, keepdims=True))
        weights = jnp.exp2(scores - now[:, 0:1]).astype(jnp.bfloat16)
        added = jnp.dot(weights, values, preferred_element_type=jnp.float32)
        keep = jnp.exp2(before - now)
        top[rows, :] = now
        acc[rows, 0:HD] = acc[rows, 0:HD] * keep + added[:, 0:HD]
        acc[rows, HD:2 * HD] = acc[rows, HD:2 * HD] * keep + added[:, HD:2 * HD]

    def score(n, keys):
        return lax.dot_general(
            q2[n * ROWS:(n + 1) * ROWS, :], keys, (((1,), (1,)), ((), ())),
            preferred_element_type=jnp.float32)

    def load_window():
        halos[1].wait_recv()
        rows = slice(BLK, WINDOW)
        wk[rows, 0:HD] = window[rows, 0:HD]
        lane = lax.broadcasted_iota(jnp.int32, (WINDOW - BLK, HD), 1)
        wk[rows, HD:2 * HD] = jnp.where(
            lane == HD - 1, jnp.zeros((WINDOW - BLK, HD), jnp.bfloat16), window[rows, 0:HD])
        wv[rows, 0:HD] = window[rows, HD:2 * HD]

    def slash(n):
        place = core if n < NY else other
        first = ((y + n % NY) % NY) * SUB
        block = 2 * place + first // BLK
        keys = pl.ds(pl.multiple_of((block + 1) * BLK, BLK), 8 * BLK)
        column = lax.broadcasted_iota(jnp.int32, (ROWS, 8 * BLK), 1)
        token = lax.broadcasted_iota(jnp.int32, (ROWS, 8 * BLK), 0) % SUB + first % BLK
        allowed = (column <= 7 * BLK + token) & (column >= (7 - block - 4 * chip) * BLK)
        scores = jnp.where(allowed, score(n, wk[keys, :]), FLOOR)
        update(n, scores, wv[keys, :])

    def load_tile(k):
        row = row_of(k)
        lane = lax.broadcasted_iota(jnp.int32, (BLK, HD), 1)
        for cx in range(NX):
            for b in range(4):
                owner = 2 * (cx * NZ + row) + b // 2
                fill = jnp.broadcast_to(bias[b % 2, pl.ds(owner, 1), :], (BLK, HD))
                rows = slice(b * BLK, (b + 1) * BLK)
                there = slice(cx * CHUNK_KEYS + b * BLK, cx * CHUNK_KEYS + (b + 1) * BLK)
                keys = gathered[row, cx, rows, 0:HD]
                k2[there, 0:HD] = keys
                k2[there, HD:2 * HD] = jnp.where(lane == HD - 1, fill.astype(jnp.bfloat16), keys)
                v2[there, 0:HD] = gathered[row, cx, rows, HD:2 * HD]

    stage_a(1)

    def step(k, carry):
        @pl.when(k + 2 < NZ)
        def _():
            stage_a(k + 2)

        stage_b(k + 1)
        stage_c(k)

        @pl.when(k == HALO_AT)
        def _():
            swaps[2].wait_recv()
            halos[0].start()

        @pl.when(k == RELAY_AT)
        def _():
            halos[0].wait_recv()
            halos[1].start()
        load_tile(k)
        for n in range(CHUNKS):
            update(n, score(n, k2[...]), v2[...])
        return carry

    lax.fori_loop(0, NZ - 1, step, 0)
    stage_c(NZ - 1)
    load_tile(NZ - 1)
    load_window()
    pl.semaphore_wait(ready.at[1], 1)

    out_columns = pl.ds(pl.multiple_of(y * 2 * QW + core * QW, QW), QW)
    sends = []
    keep_own = pltpu.make_async_copy(slab.at[0], out_hbm.at[:, out_columns], own_sem)
    for n in (2, 6, 1, 5, 3, 7, 4, 0):
        update(n, score(n, k2[...]), v2[...])
        slash(n)
        rows = slice(n * ROWS, (n + 1) * ROWS)
        done = (acc[rows, 0:HD] / acc[rows, HD:2 * HD]).astype(jnp.bfloat16)
        for h in range(GROUP):
            slab[n, :, h * HD:(h + 1) * HD] = done[h * SUB:(h + 1) * SUB, :]
        if n == 0:
            keep_own.start()
        else:
            place = core if n < NY else other
            send = remote(slab.at[n], out_hbm.at[:, out_columns], out_send.at[n], out_recv.at[n],
                          (2 * chip + place, (y + n % NY) % NY))
            send.start()
            sends.append(send)

    for swap in swaps:
        swap.wait_send()
    for halo in halos:
        halo.wait_send()

    def finish(k, carry):
        along_z(k, 0, drain)

        @pl.when((k == 0) | column_first(k))
        def _():
            along_x(k, drain)

        @pl.when(column_first(k))
        def _():
            relay_x(k, drain)

        @pl.when(jnp.logical_not(column_first(k)))
        def _():
            for off in (1, 2, 3):
                along_z(k, off, drain)
        return carry

    lax.fori_loop(0, NZ, finish, 0)
    for send in sends:
        send.wait()
    keep_own.wait()


def body(queries, span_kv, cache_kv, verticals, offsets):
    cache_blocks = cache_kv.shape[0] // BLK
    bf16 = jnp.bfloat16
    any_space = pl.BlockSpec(memory_space=pl.ANY)
    dma = pltpu.SemaphoreType.DMA
    return pl.pallas_call(
        kernel,
        out_shape=jax.ShapeDtypeStruct((SUB, 4 * 2 * QW), bf16),
        in_specs=[any_space] * 4,
        out_specs=any_space,
        scratch_shapes=[
            pltpu.VMEM((2, NV), jnp.int32),
            pltpu.VMEM((2, 2 * CHIPS, HD), jnp.float32),
            pltpu.VMEM((cache_blocks, BLK) + cache_kv.shape[1:], bf16),
            pltpu.VMEM(span_kv.shape, bf16),
            pltpu.VMEM((2, TOK, 2 * HD), bf16),
            pltpu.VMEM((2, 2 * BLK, 2 * HD), bf16),
            pltpu.VMEM((NZ, NX, CHUNK_KEYS, 2 * HD), bf16),
            pltpu.VMEM((TOK, QW), bf16),
            pltpu.VMEM((TOK, QW), bf16),
            pltpu.VMEM((WINDOW, 2 * HD), bf16),
            pltpu.VMEM((CHUNKS * ROWS, 2 * HD), bf16),
            pltpu.VMEM((TILE, 2 * HD), bf16),
            pltpu.VMEM((TILE, 2 * HD), bf16),
            pltpu.VMEM((WINDOW, 2 * HD), bf16),
            pltpu.VMEM((WINDOW, 2 * HD), bf16),
            pltpu.VMEM((CHUNKS * ROWS, 2 * HD), jnp.float32),
            pltpu.VMEM((CHUNKS * ROWS, HD), jnp.float32),
            pltpu.VMEM((CHUNKS, SUB, QW), bf16),
            dma((4,)), dma((3,)), dma((3,)), dma((2,)), dma((2,)), pltpu.SemaphoreType.REGULAR((2,)),
            dma((NZ, NX, 5)), dma((NZ, NX)), dma((CHUNKS,)), dma((CHUNKS,)), dma,
        ],
        compiler_params=pltpu.CompilerParams(
            collective_id=0, has_side_effects=True, vmem_limit_bytes=60 << 20),
    )(verticals, queries, span_kv, cache_kv.reshape((cache_blocks, BLK) + cache_kv.shape[1:]))


def solution(mesh):
    in_specs = (
        P("ctx", "head"),
        P("ctx", "head", None),
        P("ctx", "head", None),
        P("head", None),
        P("head", None),
    )
    out_specs = P(("ctx", "head"), None)
    return jax.shard_map(body, mesh=mesh, in_specs=in_specs, out_specs=out_specs, check_vma=False)
```

```python
import jax
import jax.numpy as jnp
from jax import lax
from jax.experimental import pallas as pl
from jax.experimental.pallas import tpu as pltpu
from jax.sharding import PartitionSpec as P

BLK = 64
HD = 128
NX, NZ, NY = 4, 8, 4
CHIPS = NX * NZ
GROUP = 8
TOK = 128
SUB = TOK // NY
ROWS = GROUP * SUB
CHUNKS = 2 * NY
CHUNK_KEYS = 4 * BLK
TILE = NX * CHUNK_KEYS
FAR = 2 * TOK
WINDOW = 3 * FAR
NV = 64
HALO_AT, RELAY_AT = 0, 2
QW = GROUP * HD
FLOOR = -1e30
DEAD = -30000.0
SCALE = float(HD ** -0.5 * 1.4426950408889634)
MESH = pl.DeviceIdType.MESH


def kernel(verts_hbm, q_hbm, span_hbm, cache_hbm, out_hbm,
           verts, bias, cache, span, span_heads, staged, gathered, q_own, q_far, window,
           q2, k2, v2, wk, wv, acc, top, slab,
           load_sem, swap_send, swap_recv, halo_send, halo_recv, ready,
           piece_send, piece_recv, out_send, out_recv, own_sem):
    me = lax.axis_index("ctx")
    y = lax.axis_index("head")
    chip = me // 2
    core = me % 2
    other = 1 - core
    x = chip // NZ
    z = chip % NZ

    def at_chip(cx, cz, which):
        return (2 * ((cx % NX) * NZ + cz % NZ) + which, y)

    partner = (2 * chip + other, y)
    x_up, x_down, x_far = (at_chip(x + s, z, core) for s in (1, NX - 1, 2))
    z_up, z_down = (at_chip(x, z + s, core) for s in (1, NZ - 1))
    after, before_it = ((2 * ((chip + CHIPS + s) % CHIPS) + core, y) for s in (1, -1))

    load_verts = pltpu.make_async_copy(verts_hbm, verts, load_sem.at[3])
    load_verts.start()
    barrier = pltpu.get_barrier_semaphore()
    peers = [partner, x_up, x_down, z_up, z_down, after, before_it]
    peers += [(2 * chip + w, (y + r) % NY) for r in (1, 3) for w in (0, 1)]
    for peer in peers:
        pl.semaphore_signal(barrier, inc=1, device_id=peer, device_id_type=MESH)

    load_cache = pltpu.make_async_copy(cache_hbm, cache, load_sem.at[0])
    load_span = pltpu.make_async_copy(span_hbm, span, load_sem.at[1])
    own_columns = pl.ds(pl.multiple_of(core * QW, QW), QW)
    far_columns = pl.ds(pl.multiple_of(other * QW, QW), QW)
    load_q = pltpu.make_async_copy(q_hbm.at[:, own_columns], q_own, load_sem.at[2])
    load_span.start()
    load_cache.start()
    load_q.start()

    load_verts.wait()
    mine_at = (verts[...] // BLK) == me
    within = verts[...] % BLK
    most = jnp.where(mine_at, within, 0)
    least = jnp.where(mine_at, within, BLK - 1)
    owner_row = verts[pl.ds(core, 1), :] // BLK
    owner_index = lax.broadcasted_iota(jnp.int32, (2 * CHIPS, NV), 0)
    held = jnp.sum(jnp.where(owner_index == owner_row, 1.0, 0.0), axis=1, keepdims=True)
    for slot in range(2):
        dead = jnp.where(held > slot + 0.5, 0.0, DEAD)
        bias[slot] = jnp.broadcast_to(dead, (2 * CHIPS, HD))
    load_span.wait()
    both = span[...].astype(jnp.float32)
    for head in range(2):
        span_heads[head] = both[:, head, :].astype(jnp.bfloat16)
    load_cache.wait()
    for head in range(2):
        for slot in range(2):
            pick = jnp.max(most[head:head + 1]) if slot == 0 else jnp.min(least[head:head + 1])
            block = cache[pick].astype(jnp.float32)
            staged[head, slot * BLK:(slot + 1) * BLK, :] = block[:, head, :].astype(jnp.bfloat16)

    mine = pl.ds(pl.multiple_of(core * 2 * BLK, 2 * BLK), 2 * BLK)
    gathered[z, x, mine, :] = staged[core]
    own_rows = pl.ds(pl.multiple_of(4 * TOK + core * TOK, TOK), TOK)
    window[own_rows, :] = span_heads[core]

    pl.semaphore_wait(barrier, len(peers))
    pl.semaphore_signal(ready.at[0], inc=1, device_id=x_up, device_id_type=MESH)
    pl.semaphore_signal(ready.at[1], inc=1, device_id=(me, (y + 1) % NY), device_id_type=MESH)

    def remote(src, dst, send, recv, device):
        return pltpu.make_async_remote_copy(
            src_ref=src, dst_ref=dst, send_sem=send, recv_sem=recv,
            device_id=device, device_id_type=MESH)

    swaps = [
        remote(staged.at[other], gathered.at[z, x, mine, :], swap_send.at[0], swap_recv.at[0], partner),
        remote(q_hbm.at[:, far_columns], q_far, swap_send.at[1], swap_recv.at[1], partner),
        remote(span_heads.at[other], window.at[own_rows, :], swap_send.at[2], swap_recv.at[2], partner),
    ]
    for swap in swaps:
        swap.start()
    halos = [
        remote(window.at[2 * FAR:3 * FAR, :], window.at[FAR:2 * FAR, :],
               halo_send.at[0], halo_recv.at[0], after),
        remote(window.at[FAR + BLK:2 * FAR, :], window.at[BLK:FAR, :],
               halo_send.at[1], halo_recv.at[1], after),
    ]

    def row_of(k):
        return (z + NZ + (1 - 2 * (k % 2)) * ((k + 1) // 2)) % NZ

    def piece(k, off, way, device, k_there, off_there):
        src = gathered.at[row_of(k), (x + off) % NX]
        return remote(src, src, piece_send.at[k, off, way],
                      piece_recv.at[k_there, off_there], device)

    def along_z(k, off, act):
        last_up, last_down = (3, 6) if off == 0 else (1, 4)

        @pl.when(k == 0)
        def _():
            act(piece(k, off, 0, z_up, 1, off))
            act(piece(k, off, 1, z_down, 2, off))

        @pl.when((k % 2 == 1) & (k <= last_up))
        def _():
            act(piece(k, off, 0, z_up, k + 2, off))

        @pl.when((k % 2 == 0) & (k >= 2) & (k <= last_down))
        def _():
            act(piece(k, off, 1, z_down, k + 2 - k // 6, off))

    def along_x(k, act):
        act(piece(k, 0, 2, x_up, k, 3))
        act(piece(k, 0, 3, x_down, k, 1))

        @pl.when((k == 0) & (core == 0))
        def _():
            act(piece(k, 0, 4, x_far, k, 2))

    def relays_up(k):
        return (k % 2 == 1) & (k < 7)

    def relays_down(k):
        return (k % 2 == 0) | (k == 7)

    def relay_x(k, act):
        @pl.when(relays_up(k))
        def _():
            act(piece(k, 3, 2, x_up, k, 2))

        @pl.when(relays_down(k))
        def _():
            act(piece(k, 1, 3, x_down, k, 2))

    def column_first(k):
        return (core == 1) | (k == 5) | (k == 7)

    def begin(copy):
        copy.start()

    def drain(copy):
        copy.wait_send()

    def arrive(k, off):
        here = gathered.at[row_of(k), (x + off) % NX]
        remote(here, here, piece_send.at[k, off, 0], piece_recv.at[k, off], partner).wait_recv()

    def stage_a(k):
        arrive(k, 0)
        along_z(k, 0, begin)

        @pl.when(column_first(k))
        def _():
            along_x(k, begin)

    def stage_b(k):
        @pl.when(column_first(k))
        def _():
            @pl.when(relays_up(k))
            def _():
                arrive(k, 3)

            @pl.when(relays_down(k))
            def _():
                arrive(k, 1)
            relay_x(k, begin)

    def stage_c(k):
        @pl.when(column_first(k))
        def _():
            @pl.when(relays_up(k))
            def _():
                arrive(k, 1)

            @pl.when(relays_down(k))
            def _():
                arrive(k, 3)
            arrive(k, 2)

        @pl.when(jnp.logical_not(column_first(k)))
        def _():
            for off in (1, 3, 2):
                arrive(k, off)
                along_z(k, off, begin)

    swaps[0].wait_recv()
    pl.semaphore_wait(ready.at[0], 1)
    along_z(0, 0, begin)
    along_x(0, begin)

    load_q.wait()
    swaps[1].wait_recv()
    for rel in range(2):
        source = q_own if rel == 0 else q_far
        for r in range(NY):
            first = pl.multiple_of(((y + r) % NY) * SUB, SUB)
            for h in range(GROUP):
                part = source[pl.ds(first, SUB), h * HD:(h + 1) * HD].astype(jnp.float32) * SCALE
                high = part.astype(jnp.bfloat16)
                low = (part - high.astype(jnp.float32)).astype(jnp.bfloat16)
                lane = lax.broadcasted_iota(jnp.int32, (SUB, HD), 1)
                low = jnp.where(lane == HD - 1, jnp.ones_like(low), low)
                base = (rel * NY + r) * ROWS + h * SUB
                q2[base:base + SUB, 0:HD] = high
                q2[base:base + SUB, HD:2 * HD] = low

    acc[...] = jnp.zeros_like(acc)
    top[...] = jnp.full_like(top, FLOOR)
    v2[:, HD:2 * HD] = jnp.ones((TILE, HD), jnp.bfloat16)
    wv[:, HD:2 * HD] = jnp.ones((WINDOW, HD), jnp.bfloat16)

    def update(n, scores, values):
        rows = slice(n * ROWS, (n + 1) * ROWS)
        before = top[rows, :]
        now = jnp.maximum(before, jnp.max(scores, axis=1, keepdims=True))
        weights = jnp.exp2(scores - now[:, 0:1]).astype(jnp.bfloat16)
        added = jnp.dot(weights, values, preferred_element_type=jnp.float32)
        keep = jnp.exp2(before - now)
        top[rows, :] = now
        acc[rows, 0:HD] = acc[rows, 0:HD] * keep + added[:, 0:HD]
        acc[rows, HD:2 * HD] = acc[rows, HD:2 * HD] * keep + added[:, HD:2 * HD]

    def score(n, keys):
        return lax.dot_general(
            q2[n * ROWS:(n + 1) * ROWS, :], keys, (((1,), (1,)), ((), ())),
            preferred_element_type=jnp.float32)

    def load_window():
        halos[1].wait_recv()
        rows = slice(BLK, WINDOW)
        wk[rows, 0:HD] = window[rows, 0:HD]
        lane = lax.broadcasted_iota(jnp.int32, (WINDOW - BLK, HD), 1)
        wk[rows, HD:2 * HD] = jnp.where(
            lane == HD - 1, jnp.zeros((WINDOW - BLK, HD), jnp.bfloat16), window[rows, 0:HD])
        wv[rows, 0:HD] = window[rows, HD:2 * HD]

    def slash(n):
        place = core if n < NY else other
        first = ((y + n % NY) % NY) * SUB
        block = 2 * place + first // BLK
        keys = pl.ds(pl.multiple_of((block + 1) * BLK, BLK), 8 * BLK)
        column = lax.broadcasted_iota(jnp.int32, (ROWS, 8 * BLK), 1)
        token = lax.broadcasted_iota(jnp.int32, (ROWS, 8 * BLK), 0) % SUB + first % BLK
        allowed = (column <= 7 * BLK + token) & (column >= (7 - block - 4 * chip) * BLK)
        scores = jnp.where(allowed, score(n, wk[keys, :]), FLOOR)
        update(n, scores, wv[keys, :])

    def load_tile(k):
        row = row_of(k)
        lane = lax.broadcasted_iota(jnp.int32, (BLK, HD), 1)
        for cx in range(NX):
            for b in range(4):
                owner = 2 * (cx * NZ + row) + b // 2
                fill = jnp.broadcast_to(bias[b % 2, pl.ds(owner, 1), :], (BLK, HD))
                rows = slice(b * BLK, (b + 1) * BLK)
                there = slice(cx * CHUNK_KEYS + b * BLK, cx * CHUNK_KEYS + (b + 1) * BLK)
                keys = gathered[row, cx, rows, 0:HD]
                k2[there, 0:HD] = keys
                k2[there, HD:2 * HD] = jnp.where(lane == HD - 1, fill.astype(jnp.bfloat16), keys)
                v2[there, 0:HD] = gathered[row, cx, rows, HD:2 * HD]

    stage_a(1)
    stage_b(0)

    def step(k, carry):
        @pl.when(k + 2 < NZ)
        def _():
            stage_a(k + 2)

        stage_b(k + 1)
        stage_c(k)

        @pl.when(k == HALO_AT)
        def _():
            swaps[2].wait_recv()
            halos[0].start()

        @pl.when(k == RELAY_AT)
        def _():
            halos[0].wait_recv()
            halos[1].start()
        load_tile(k)
        for n in range(CHUNKS):
            update(n, score(n, k2[...]), v2[...])
        return carry

    lax.fori_loop(0, NZ - 1, step, 0)
    stage_c(NZ - 1)
    load_tile(NZ - 1)
    load_window()
    pl.semaphore_wait(ready.at[1], 1)

    out_columns = pl.ds(pl.multiple_of(y * 2 * QW + core * QW, QW), QW)
    sends = []
    keep_own = pltpu.make_async_copy(slab.at[0], out_hbm.at[:, out_columns], own_sem)
    for n in (2, 6, 1, 5, 3, 7, 4, 0):
        update(n, score(n, k2[...]), v2[...])
        slash(n)
        rows = slice(n * ROWS, (n + 1) * ROWS)
        done = (acc[rows, 0:HD] / acc[rows, HD:2 * HD]).astype(jnp.bfloat16)
        for h in range(GROUP):
            slab[n, :, h * HD:(h + 1) * HD] = done[h * SUB:(h + 1) * SUB, :]
        if n == 0:
            keep_own.start()
        else:
            place = core if n < NY else other
            send = remote(slab.at[n], out_hbm.at[:, out_columns], out_send.at[n], out_recv.at[n],
                          (2 * chip + place, (y + n % NY) % NY))
            send.start()
            sends.append(send)

    for swap in swaps:
        swap.wait_send()
    for halo in halos:
        halo.wait_send()

    def finish(k, carry):
        along_z(k, 0, drain)

        @pl.when((k == 0) | column_first(k))
        def _():
            along_x(k, drain)

        @pl.when(column_first(k))
        def _():
            relay_x(k, drain)

        @pl.when(jnp.logical_not(column_first(k)))
        def _():
            for off in (1, 2, 3):
                along_z(k, off, drain)
        return carry

    lax.fori_loop(0, NZ, finish, 0)
    for send in sends:
        send.wait()
    keep_own.wait()


def body(queries, span_kv, cache_kv, verticals, offsets):
    cache_blocks = cache_kv.shape[0] // BLK
    bf16 = jnp.bfloat16
    any_space = pl.BlockSpec(memory_space=pl.ANY)
    dma = pltpu.SemaphoreType.DMA
    return pl.pallas_call(
        kernel,
        out_shape=jax.ShapeDtypeStruct((SUB, 4 * 2 * QW), bf16),
        in_specs=[any_space] * 4,
        out_specs=any_space,
        scratch_shapes=[
            pltpu.VMEM((2, NV), jnp.int32),
            pltpu.VMEM((2, 2 * CHIPS, HD), jnp.float32),
            pltpu.VMEM((cache_blocks, BLK) + cache_kv.shape[1:], bf16),
            pltpu.VMEM(span_kv.shape, bf16),
            pltpu.VMEM((2, TOK, 2 * HD), bf16),
            pltpu.VMEM((2, 2 * BLK, 2 * HD), bf16),
            pltpu.VMEM((NZ, NX, CHUNK_KEYS, 2 * HD), bf16),
            pltpu.VMEM((TOK, QW), bf16),
            pltpu.VMEM((TOK, QW), bf16),
            pltpu.VMEM((WINDOW, 2 * HD), bf16),
            pltpu.VMEM((CHUNKS * ROWS, 2 * HD), bf16),
            pltpu.VMEM((TILE, 2 * HD), bf16),
            pltpu.VMEM((TILE, 2 * HD), bf16),
            pltpu.VMEM((WINDOW, 2 * HD), bf16),
            pltpu.VMEM((WINDOW, 2 * HD), bf16),
            pltpu.VMEM((CHUNKS * ROWS, 2 * HD), jnp.float32),
            pltpu.VMEM((CHUNKS * ROWS, HD), jnp.float32),
            pltpu.VMEM((CHUNKS, SUB, QW), bf16),
            dma((4,)), dma((3,)), dma((3,)), dma((2,)), dma((2,)), pltpu.SemaphoreType.REGULAR((2,)),
            dma((NZ, NX, 5)), dma((NZ, NX)), dma((CHUNKS,)), dma((CHUNKS,)), dma,
        ],
        compiler_params=pltpu.CompilerParams(
            collective_id=0, has_side_effects=True, vmem_limit_bytes=60 << 20),
    )(verticals, queries, span_kv, cache_kv.reshape((cache_blocks, BLK) + cache_kv.shape[1:]))


def solution(mesh):
    in_specs = (
        P("ctx", "head"),
        P("ctx", "head", None),
        P("ctx", "head", None),
        P("head", None),
        P("head", None),
    )
    out_specs = P(("ctx", "head"), None)
    return jax.shard_map(body, mesh=mesh, in_specs=in_specs, out_specs=out_specs, check_vma=False)
```

```python
import jax
import jax.numpy as jnp
from jax import lax
from jax.experimental import pallas as pl
from jax.experimental.pallas import tpu as pltpu
from jax.sharding import PartitionSpec as P

BLK = 64
HD = 128
NX, NZ, NY = 4, 8, 4
CHIPS = NX * NZ
GROUP = 8
TOK = 128
SUB = TOK // NY
ROWS = GROUP * SUB
CHUNKS = 2 * NY
CHUNK_KEYS = 4 * BLK
TILE = NX * CHUNK_KEYS
FAR = 2 * TOK
WINDOW = 3 * FAR
NV = 64
HALO_AT, RELAY_AT = 1, 3
QW = GROUP * HD
FLOOR = -1e30
DEAD = -30000.0
SCALE = float(HD ** -0.5 * 1.4426950408889634)
MESH = pl.DeviceIdType.MESH


def kernel(verts_hbm, q_hbm, span_hbm, cache_hbm, out_hbm,
           verts, bias, cache, span, span_heads, staged, gathered, q_own, q_far, window,
           q2, k2, v2, wk, wv, acc, top, slab,
           load_sem, swap_send, swap_recv, halo_send, halo_recv, ready,
           piece_send, piece_recv, out_send, out_recv, own_sem):
    me = lax.axis_index("ctx")
    y = lax.axis_index("head")
    chip = me // 2
    core = me % 2
    other = 1 - core
    x = chip // NZ
    z = chip % NZ

    def at_chip(cx, cz, which):
        return (2 * ((cx % NX) * NZ + cz % NZ) + which, y)

    partner = (2 * chip + other, y)
    x_up, x_down, x_far = (at_chip(x + s, z, core) for s in (1, NX - 1, 2))
    z_up, z_down = (at_chip(x, z + s, core) for s in (1, NZ - 1))
    after, before_it = ((2 * ((chip + CHIPS + s) % CHIPS) + core, y) for s in (1, -1))

    load_verts = pltpu.make_async_copy(verts_hbm, verts, load_sem.at[3])
    load_verts.start()
    barrier = pltpu.get_barrier_semaphore()
    peers = [partner, x_up, x_down, z_up, z_down, after, before_it]
    peers += [(2 * chip + w, (y + r) % NY) for r in (1, 3) for w in (0, 1)]
    for peer in peers:
        pl.semaphore_signal(barrier, inc=1, device_id=peer, device_id_type=MESH)

    load_cache = pltpu.make_async_copy(cache_hbm, cache, load_sem.at[0])
    load_span = pltpu.make_async_copy(span_hbm, span, load_sem.at[1])
    own_columns = pl.ds(pl.multiple_of(core * QW, QW), QW)
    far_columns = pl.ds(pl.multiple_of(other * QW, QW), QW)
    load_q = pltpu.make_async_copy(q_hbm.at[:, own_columns], q_own, load_sem.at[2])
    load_span.start()
    load_cache.start()
    load_q.start()

    load_verts.wait()
    mine_at = (verts[...] // BLK) == me
    within = verts[...] % BLK
    most = jnp.where(mine_at, within, 0)
    least = jnp.where(mine_at, within, BLK - 1)
    owner_row = verts[pl.ds(core, 1), :] // BLK
    owner_index = lax.broadcasted_iota(jnp.int32, (2 * CHIPS, NV), 0)
    held = jnp.sum(jnp.where(owner_index == owner_row, 1.0, 0.0), axis=1, keepdims=True)
    for slot in range(2):
        dead = jnp.where(held > slot + 0.5, 0.0, DEAD)
        bias[slot] = jnp.broadcast_to(dead, (2 * CHIPS, HD))
    load_span.wait()
    both = span[...].astype(jnp.float32)
    for head in range(2):
        span_heads[head] = both[:, head, :].astype(jnp.bfloat16)
    load_cache.wait()
    for head in range(2):
        for slot in range(2):
            pick = jnp.max(most[head:head + 1]) if slot == 0 else jnp.min(least[head:head + 1])
            block = cache[pick].astype(jnp.float32)
            staged[head, slot * BLK:(slot + 1) * BLK, :] = block[:, head, :].astype(jnp.bfloat16)

    mine = pl.ds(pl.multiple_of(core * 2 * BLK, 2 * BLK), 2 * BLK)
    gathered[z, x, mine, :] = staged[core]
    own_rows = pl.ds(pl.multiple_of(4 * TOK + core * TOK, TOK), TOK)
    window[own_rows, :] = span_heads[core]

    pl.semaphore_wait(barrier, len(peers))
    pl.semaphore_signal(ready.at[0], inc=1, device_id=x_up, device_id_type=MESH)
    pl.semaphore_signal(ready.at[1], inc=1, device_id=(me, (y + 1) % NY), device_id_type=MESH)

    def remote(src, dst, send, recv, device):
        return pltpu.make_async_remote_copy(
            src_ref=src, dst_ref=dst, send_sem=send, recv_sem=recv,
            device_id=device, device_id_type=MESH)

    swaps = [
        remote(staged.at[other], gathered.at[z, x, mine, :], swap_send.at[0], swap_recv.at[0], partner),
        remote(q_hbm.at[:, far_columns], q_far, swap_send.at[1], swap_recv.at[1], partner),
        remote(span_heads.at[other], window.at[own_rows, :], swap_send.at[2], swap_recv.at[2], partner),
    ]
    for swap in swaps:
        swap.start()
    halos = [
        remote(window.at[2 * FAR:3 * FAR, :], window.at[FAR:2 * FAR, :],
               halo_send.at[0], halo_recv.at[0], after),
        remote(window.at[FAR + BLK:2 * FAR, :], window.at[BLK:FAR, :],
               halo_send.at[1], halo_recv.at[1], after),
    ]

    def row_of(k):
        return (z + NZ + (1 - 2 * (k % 2)) * ((k + 1) // 2)) % NZ

    def piece(k, off, way, device, k_there, off_there):
        src = gathered.at[row_of(k), (x + off) % NX]
        return remote(src, src, piece_send.at[k, off, way],
                      piece_recv.at[k_there, off_there], device)

    def along_z(k, off, act):
        last_up, last_down = (3, 6) if off == 0 else (1, 4)

        @pl.when(k == 0)
        def _():
            act(piece(k, off, 0, z_up, 1, off))
            act(piece(k, off, 1, z_down, 2, off))

        @pl.when((k % 2 == 1) & (k <= last_up))
        def _():
            act(piece(k, off, 0, z_up, k + 2, off))

        @pl.when((k % 2 == 0) & (k >= 2) & (k <= last_down))
        def _():
            act(piece(k, off, 1, z_down, k + 2 - k // 6, off))

    def along_x(k, act):
        act(piece(k, 0, 2, x_up, k, 3))
        act(piece(k, 0, 3, x_down, k, 1))

        @pl.when((k == 0) & (core == 0))
        def _():
            act(piece(k, 0, 4, x_far, k, 2))

    def relays_up(k):
        return (k % 2 == 1) & (k < 7)

    def relays_down(k):
        return (k % 2 == 0) | (k == 7)

    def relay_x(k, act):
        @pl.when(relays_up(k))
        def _():
            act(piece(k, 3, 2, x_up, k, 2))

        @pl.when(relays_down(k))
        def _():
            act(piece(k, 1, 3, x_down, k, 2))

    def column_first(k):
        return (core == 1) | (k == 5) | (k == 7)

    def begin(copy):
        copy.start()

    def drain(copy):
        copy.wait_send()

    def arrive(k, off):
        here = gathered.at[row_of(k), (x + off) % NX]
        remote(here, here, piece_send.at[k, off, 0], piece_recv.at[k, off], partner).wait_recv()

    def stage_a(k):
        arrive(k, 0)
        along_z(k, 0, begin)

        @pl.when(column_first(k))
        def _():
            along_x(k, begin)

    def stage_b(k):
        @pl.when(column_first(k))
        def _():
            @pl.when(relays_up(k))
            def _():
                arrive(k, 3)

            @pl.when(relays_down(k))
            def _():
                arrive(k, 1)
            relay_x(k, begin)

    def stage_c(k):
        @pl.when(column_first(k))
        def _():
            @pl.when(relays_up(k))
            def _():
                arrive(k, 1)

            @pl.when(relays_down(k))
            def _():
                arrive(k, 3)
            arrive(k, 2)

        @pl.when(jnp.logical_not(column_first(k)))
        def _():
            for off in (1, 3, 2):
                arrive(k, off)
                along_z(k, off, begin)

    swaps[0].wait_recv()
    pl.semaphore_wait(ready.at[0], 1)
    along_z(0, 0, begin)
    along_x(0, begin)

    load_q.wait()
    swaps[1].wait_recv()
    for rel in range(2):
        source = q_own if rel == 0 else q_far
        for r in range(NY):
            first = pl.multiple_of(((y + r) % NY) * SUB, SUB)
            for h in range(GROUP):
                part = source[pl.ds(first, SUB), h * HD:(h + 1) * HD].astype(jnp.float32) * SCALE
                high = part.astype(jnp.bfloat16)
                low = (part - high.astype(jnp.float32)).astype(jnp.bfloat16)
                lane = lax.broadcasted_iota(jnp.int32, (SUB, HD), 1)
                low = jnp.where(lane == HD - 1, jnp.ones_like(low), low)
                base = (rel * NY + r) * ROWS + h * SUB
                q2[base:base + SUB, 0:HD] = high
                q2[base:base + SUB, HD:2 * HD] = low

    acc[...] = jnp.zeros_like(acc)
    top[...] = jnp.full_like(top, FLOOR)
    v2[:, HD:2 * HD] = jnp.ones((TILE, HD), jnp.bfloat16)
    wv[:, HD:2 * HD] = jnp.ones((WINDOW, HD), jnp.bfloat16)

    def update(n, scores, values):
        rows = slice(n * ROWS, (n + 1) * ROWS)
        before = top[rows, :]
        now = jnp.maximum(before, jnp.max(scores, axis=1, keepdims=True))
        weights = jnp.exp2(scores - now[:, 0:1]).astype(jnp.bfloat16)
        added = jnp.dot(weights, values, preferred_element_type=jnp.float32)
        keep = jnp.exp2(before - now)
        top[rows, :] = now
        acc[rows, 0:HD] = acc[rows, 0:HD] * keep + added[:, 0:HD]
        acc[rows, HD:2 * HD] = acc[rows, HD:2 * HD] * keep + added[:, HD:2 * HD]

    def score(n, keys):
        return lax.dot_general(
            q2[n * ROWS:(n + 1) * ROWS, :], keys, (((1,), (1,)), ((), ())),
            preferred_element_type=jnp.float32)

    def load_window():
        halos[1].wait_recv()
        rows = slice(BLK, WINDOW)
        wk[rows, 0:HD] = window[rows, 0:HD]
        lane = lax.broadcasted_iota(jnp.int32, (WINDOW - BLK, HD), 1)
        wk[rows, HD:2 * HD] = jnp.where(
            lane == HD - 1, jnp.zeros((WINDOW - BLK, HD), jnp.bfloat16), window[rows, 0:HD])
        wv[rows, 0:HD] = window[rows, HD:2 * HD]

    def slash(n):
        place = core if n < NY else other
        first = ((y + n % NY) % NY) * SUB
        block = 2 * place + first // BLK
        keys = pl.ds(pl.multiple_of((block + 1) * BLK, BLK), 8 * BLK)
        column = lax.broadcasted_iota(jnp.int32, (ROWS, 8 * BLK), 1)
        token = lax.broadcasted_iota(jnp.int32, (ROWS, 8 * BLK), 0) % SUB + first % BLK
        allowed = (column <= 7 * BLK + token) & (column >= (7 - block - 4 * chip) * BLK)
        scores = jnp.where(allowed, score(n, wk[keys, :]), FLOOR)
        update(n, scores, wv[keys, :])

    def load_tile(k):
        row = row_of(k)
        lane = lax.broadcasted_iota(jnp.int32, (BLK, HD), 1)
        for cx in range(NX):
            for b in range(4):
                owner = 2 * (cx * NZ + row) + b // 2
                fill = jnp.broadcast_to(bias[b % 2, pl.ds(owner, 1), :], (BLK, HD))
                rows = slice(b * BLK, (b + 1) * BLK)
                there = slice(cx * CHUNK_KEYS + b * BLK, cx * CHUNK_KEYS + (b + 1) * BLK)
                keys = gathered[row, cx, rows, 0:HD]
                k2[there, 0:HD] = keys
                k2[there, HD:2 * HD] = jnp.where(lane == HD - 1, fill.astype(jnp.bfloat16), keys)
                v2[there, 0:HD] = gathered[row, cx, rows, HD:2 * HD]

    stage_a(1)
    stage_b(0)

    def step(k, carry):
        @pl.when(k + 2 < NZ)
        def _():
            stage_a(k + 2)

        stage_b(k + 1)
        stage_c(k)

        @pl.when(k == HALO_AT)
        def _():
            swaps[2].wait_recv()
            halos[0].start()

        @pl.when(k == RELAY_AT)
        def _():
            halos[0].wait_recv()
            halos[1].start()
        load_tile(k)
        for n in range(CHUNKS):
            update(n, score(n, k2[...]), v2[...])
        return carry

    lax.fori_loop(0, NZ - 1, step, 0)
    stage_c(NZ - 1)
    load_tile(NZ - 1)
    load_window()
    pl.semaphore_wait(ready.at[1], 1)

    out_columns = pl.ds(pl.multiple_of(y * 2 * QW + core * QW, QW), QW)
    sends = []
    keep_own = pltpu.make_async_copy(slab.at[0], out_hbm.at[:, out_columns], own_sem)
    for n in (2, 6, 1, 5, 3, 7, 4, 0):
        update(n, score(n, k2[...]), v2[...])
        slash(n)
        rows = slice(n * ROWS, (n + 1) * ROWS)
        done = (acc[rows, 0:HD] / acc[rows, HD:2 * HD]).astype(jnp.bfloat16)
        for h in range(GROUP):
            slab[n, :, h * HD:(h + 1) * HD] = done[h * SUB:(h + 1) * SUB, :]
        if n == 0:
            keep_own.start()
        else:
            place = core if n < NY else other
            send = remote(slab.at[n], out_hbm.at[:, out_columns], out_send.at[n], out_recv.at[n],
                          (2 * chip + place, (y + n % NY) % NY))
            send.start()
            sends.append(send)

    for swap in swaps:
        swap.wait_send()
    for halo in halos:
        halo.wait_send()

    def finish(k, carry):
        along_z(k, 0, drain)

        @pl.when((k == 0) | column_first(k))
        def _():
            along_x(k, drain)

        @pl.when(column_first(k))
        def _():
            relay_x(k, drain)

        @pl.when(jnp.logical_not(column_first(k)))
        def _():
            for off in (1, 2, 3):
                along_z(k, off, drain)
        return carry

    lax.fori_loop(0, NZ, finish, 0)
    for send in sends:
        send.wait()
    keep_own.wait()


def body(queries, span_kv, cache_kv, verticals, offsets):
    cache_blocks = cache_kv.shape[0] // BLK
    bf16 = jnp.bfloat16
    any_space = pl.BlockSpec(memory_space=pl.ANY)
    dma = pltpu.SemaphoreType.DMA
    return pl.pallas_call(
        kernel,
        out_shape=jax.ShapeDtypeStruct((SUB, 4 * 2 * QW), bf16),
        in_specs=[any_space] * 4,
        out_specs=any_space,
        scratch_shapes=[
            pltpu.VMEM((2, NV), jnp.int32),
            pltpu.VMEM((2, 2 * CHIPS, HD), jnp.float32),
            pltpu.VMEM((cache_blocks, BLK) + cache_kv.shape[1:], bf16),
            pltpu.VMEM(span_kv.shape, bf16),
            pltpu.VMEM((2, TOK, 2 * HD), bf16),
            pltpu.VMEM((2, 2 * BLK, 2 * HD), bf16),
            pltpu.VMEM((NZ, NX, CHUNK_KEYS, 2 * HD), bf16),
            pltpu.VMEM((TOK, QW), bf16),
            pltpu.VMEM((TOK, QW), bf16),
            pltpu.VMEM((WINDOW, 2 * HD), bf16),
            pltpu.VMEM((CHUNKS * ROWS, 2 * HD), bf16),
            pltpu.VMEM((TILE, 2 * HD), bf16),
            pltpu.VMEM((TILE, 2 * HD), bf16),
            pltpu.VMEM((WINDOW, 2 * HD), bf16),
            pltpu.VMEM((WINDOW, 2 * HD), bf16),
            pltpu.VMEM((CHUNKS * ROWS, 2 * HD), jnp.float32),
            pltpu.VMEM((CHUNKS * ROWS, HD), jnp.float32),
            pltpu.VMEM((CHUNKS, SUB, QW), bf16),
            dma((4,)), dma((3,)), dma((3,)), dma((2,)), dma((2,)), pltpu.SemaphoreType.REGULAR((2,)),
            dma((NZ, NX, 5)), dma((NZ, NX)), dma((CHUNKS,)), dma((CHUNKS,)), dma,
        ],
        compiler_params=pltpu.CompilerParams(
            collective_id=0, has_side_effects=True, vmem_limit_bytes=60 << 20),
    )(verticals, queries, span_kv, cache_kv.reshape((cache_blocks, BLK) + cache_kv.shape[1:]))


def solution(mesh):
    in_specs = (
        P("ctx", "head"),
        P("ctx", "head", None),
        P("ctx", "head", None),
        P("head", None),
        P("head", None),
    )
    out_specs = P(("ctx", "head"), None)
    return jax.shard_map(body, mesh=mesh, in_specs=in_specs, out_specs=out_specs, check_vma=False)
```
